32 devices in a mesh: tm: 8 (over z, y), space: 4 (over x, core).
Axes of the slice: x: 2, y: 2, z: 4, core: 2. Of those that a mesh axis runs over, the one named last changes fastest.
Arguments:
- initial_guess: float32 [8, 1024, 1024], P('tm', 'space'), may hold values from -6 to 6
- start_field: float32 [1024, 1024], P('space'), may hold values from -6 to 6
- source_field: float32 [1024, 1024], P('space'), may hold values from -0.3 to 0.3
Outputs:
- final_states: float32 [8, 1024, 1024], P('tm', 'space')
The draws below stay inside these ranges and needn't reach their ends.
All inputs are finite; a program needn't handle non-finite values.
Results may differ from the reference program's by a relative error of at most 0.00013.
Values sent between devices are 32-bit elements; how exact they have to be, the bound alone decides.
A program may use at most 64 MiB of HBM per device.

```python
import jax
import jax.numpy as jnp
from jax import lax

N = 1024
M = 16
ITERS = 1
K = 8


def levels(key, extent, split, smallest, high):
    factor_of = 1.0
    for position, shards_of in split:
        heights = jax.random.uniform(jax.random.fold_in(jax.random.fold_in(key, 6), position), (shards_of,), jnp.float32, smallest / len(split), high / len(split))
        factor_of = factor_of * jnp.repeat(jnp.exp(heights), extent[position] // shards_of).reshape((-1,) + (1,) * (len(extent) - 1 - position))
    return factor_of


def centred(own_key, shape, deviation, bound, shards=(), held_as=jnp.bfloat16):
    entries = deviation * jax.random.normal(own_key, shape, jnp.float32)
    if shards:
        entries = entries * levels(own_key, shape, shards, -0.22, 0.18)
    return jnp.clip(entries, -bound, bound).astype(held_as)


def setup_inputs(seed: int = 0) -> dict:
    arg_keys = jax.random.split(jax.random.key(seed), 4)
    return {
        "initial_guess": centred(arg_keys[0], (K, N, N), 1.0, 6.0, ((0, 8), (1, 4)), jnp.float32),
        "start_field": centred(arg_keys[1], (N, N), 1.0, 6.0, ((0, 4),), jnp.float32),
        "source_field": centred(arg_keys[2], (N, N), 0.05, 0.3, ((0, 4),), jnp.float32),
    }


decay_rate = 0.0005
spread_rate = 0.01


def mode_symbols():
    mode_index = jnp.arange(N).astype(jnp.float32)
    half_sines = jnp.sin(jnp.pi * mode_index / N) ** 2
    stiffness = 4.0 * (half_sines[:, None] + half_sines[None, :])
    fine_factor = 1.0 / (1.0 + decay_rate + spread_rate * stiffness)
    coarse_factor = 1.0 / (1.0 + M * decay_rate + M * spread_rate * stiffness)
    fine_power = jnp.ones_like(fine_factor)
    forcing_symbol = jnp.zeros_like(fine_factor)
    for substep in range(M):
        fine_power = fine_power * fine_factor
        forcing_symbol = forcing_symbol + fine_power
    return fine_power, forcing_symbol, coarse_factor


def propagate(symbol, fields):
    return jnp.real(jnp.fft.ifft2(symbol * jnp.fft.fft2(fields))).astype(jnp.float32)


def reference(initial_guess, start_field, source_field):
    fine_power, forcing_symbol, coarse_factor = mode_symbols()
    forcing = propagate(forcing_symbol, source_field)
    states = initial_guess
    for iteration in range(ITERS):
        previous = jnp.concatenate([start_field[None], states[:-1]], axis=0)
        relaxed = propagate(fine_power, previous) + forcing
        previous_relaxed = jnp.concatenate([start_field[None], relaxed[:-1]], axis=0)
        residual = propagate(fine_power, previous_relaxed) + forcing - relaxed
        residual_hat = jnp.fft.fft2(residual)

        def advance(carried, current):
            updated = coarse_factor * carried + current
            return updated, updated

        unused, errors_hat = lax.scan(advance, jnp.zeros_like(residual_hat[0]), residual_hat)
        states = relaxed + jnp.real(jnp.fft.ifft2(errors_hat)).astype(jnp.float32)
    return states
```

```python
import functools

import jax
import jax.numpy as jnp
import numpy as np
from jax import lax
from jax.experimental import pallas as pl
from jax.experimental.pallas import tpu as pltpu
from jax.sharding import PartitionSpec as P

M = 16
MESH = pl.DeviceIdType.MESH

decay_rate = 0.0005
spread_rate = 0.01


def mode_order(length):
    return np.concatenate([np.arange(0, length, 2), np.arange(1, length, 2)])


def half_kernels(length):
    half = length // 2
    product = mode_order(length)[:, None] * np.arange(half)[None, :] % length
    angles = 2.0 * np.pi / length * product
    full = (np.cos(angles) + np.sin(angles)).astype(np.float32).reshape(2, half, half)
    high = full.astype(jnp.bfloat16)
    low = (full - high.astype(np.float32)).astype(jnp.bfloat16)
    return np.stack([high, low])


def split(value):
    high = value.astype(jnp.bfloat16)
    low = (value - high.astype(jnp.float32)).astype(jnp.bfloat16)
    return high, low


def dot(a, b, transposed):
    dims = (((1,), (1 if transposed else 0,)), ((), ()))
    return lax.dot_general(a, b, dims, preferred_element_type=jnp.float32)


def dot3(a_high, a_low, b_high, b_low, transposed=False):
    return (
        dot(a_high, b_high, transposed)
        + (dot(a_low, b_high, transposed) + dot(a_high, b_low, transposed))
    )


def mgrit_kernel(
    turns, shards,
    guess, start, source, kernels_hbm, rows_hbm, columns_ref, out_ref,
    field, kernels, row_sines, sums_high, sums_low, along, gathered, spectra, states, spread, returned,
    load_sem, kernel_sem, rows_sem, send_one, recv_one, send_two, recv_two, own_sem,
):
    tm, space = lax.axis_index("tm"), lax.axis_index("space")
    devices = turns * shards
    me = tm * shards + space
    group = devices // 2
    my_half = me // group
    rows, length = field.shape
    half = length // 2
    width = length // devices

    kernel_load = pltpu.make_async_copy(kernels_hbm, kernels, kernel_sem)
    kernel_load.start()
    rows_load = pltpu.make_async_copy(
        rows_hbm.at[pl.ds(pl.multiple_of(me * width, width), width), :], row_sines, rows_sem)
    rows_load.start()

    barrier = pltpu.get_barrier_semaphore()

    def greet(step, carry):
        peer = lax.rem(me + step, devices)
        pl.semaphore_signal(barrier, inc=1, device_id=(peer // shards, lax.rem(peer, shards)), device_id_type=MESH)
        return carry

    lax.fori_loop(1, devices, greet, 0)

    @pl.when(tm < turns - 2)
    def _():
        load = pltpu.make_async_copy(guess.at[0], field, load_sem)
        load.start()
        load.wait()

    @pl.when(tm == turns - 2)
    def _():
        load = pltpu.make_async_copy(start, field, load_sem)
        load.start()
        load.wait()

    @pl.when(tm == turns - 1)
    def _():
        load = pltpu.make_async_copy(source, field, load_sem)
        load.start()
        load.wait()

    first, second = field[:, :half], field[:, half:]
    sums_high[0, :rows], sums_low[0, :rows] = split(first + second)
    sums_high[1, :rows], sums_low[1, :rows] = split(first - second)
    kernel_load.wait()

    def first_copy(peer):
        return pltpu.make_async_remote_copy(
            src_ref=along.at[pl.ds(pl.multiple_of(peer * width, width), width), :],
            dst_ref=gathered.at[space, pl.ds(pl.multiple_of(tm * width, width), width), :],
            send_sem=send_one.at[peer], recv_sem=recv_one.at[me],
            device_id=(peer // shards, lax.rem(peer, shards)), device_id_type=MESH)

    def second_copy(peer):
        turn, shard = peer // shards, lax.rem(peer, shards)
        return pltpu.make_async_remote_copy(
            src_ref=spread.at[shard, pl.ds(pl.multiple_of(turn * width, width), width), :],
            dst_ref=returned.at[pl.ds(pl.multiple_of(me * width, width), width), :],
            send_sem=send_two.at[peer], recv_sem=recv_two.at[me],
            device_id=(turn, shard), device_id_type=MESH)

    def send_half(which, copy_to):
        def send(step, carry):
            peer = which * group + lax.rem(me + step, group)

            @pl.when(peer != me)
            def _():
                copy_to(peer).start()

            return carry

        lax.fori_loop(0, group, send, 0)

    tile = min(half, 256)
    for turn in range(2):
        which = lax.rem(my_half + 1 + turn, 2)

        def row_tile(index, carry, which=which):
            offset = pl.multiple_of(index * tile, tile)
            result = dot3(
                kernels[0, which, pl.ds(offset, tile), :], kernels[1, which, pl.ds(offset, tile), :],
                sums_high[which, :rows], sums_low[which, :rows], True)
            along[pl.ds(pl.multiple_of(which * half + index * tile, tile), tile), :] = result
            return carry

        lax.fori_loop(0, half // tile, row_tile, 0)
        if turn == 0:
            pl.semaphore_wait(barrier, devices - 1)
        send_half(which, first_copy)

    own = pltpu.make_async_copy(
        along.at[pl.ds(pl.multiple_of(me * width, width), width), :],
        gathered.at[space, pl.ds(pl.multiple_of(tm * width, width), width), :], own_sem.at[0])
    own.start()
    own.wait()
    rows_load.wait()

    def arrive_one(step, carry):
        peer = lax.rem(me + step, devices)
        pltpu.make_async_remote_copy(
            src_ref=along.at[pl.ds(pl.multiple_of(me * width, width), width), :],
            dst_ref=gathered.at[lax.rem(peer, shards), pl.ds(pl.multiple_of(peer // shards * width, width), width), :],
            send_sem=send_one.at[peer], recv_sem=recv_one.at[peer],
            device_id=(peer // shards, lax.rem(peer, shards)), device_id_type=MESH).wait_recv()
        return carry

    lax.fori_loop(1, devices, arrive_one, 0)

    batch = turns * width
    for shard in range(shards // 2):
        columns = slice(shard * rows, (shard + 1) * rows)
        upper, lower = gathered[shard], gathered[shard + shards // 2]
        sums_high[0, :batch, columns], sums_low[0, :batch, columns] = split(upper + lower)
        sums_high[1, :batch, columns], sums_low[1, :batch, columns] = split(upper - lower)
    for which in range(2):
        def column_tile(index, carry, which=which):
            offset = pl.multiple_of(index * tile, tile)
            spectra[:, pl.ds(pl.multiple_of(which * half + index * tile, tile), tile)] = dot3(
                sums_high[which, :batch], sums_low[which, :batch],
                kernels[0, which, pl.ds(offset, tile), :], kernels[1, which, pl.ds(offset, tile), :], True)
            return carry

        lax.fori_loop(0, half // tile, column_tile, 0)

    lanes = 256
    scale = 1.0 / float(length * length)

    def mix(index, carry):
        row = pl.multiple_of(index // (length // lanes) * 8, 8)
        lane = pl.ds(pl.multiple_of(lax.rem(index, length // lanes) * lanes, lanes), lanes)
        row_part = jnp.concatenate([row_sines[pl.ds(row, 8), :]] * (lanes // 128), axis=1)
        stiffness = 4.0 * (columns_ref[:, lane] + row_part)
        fine_factor = 1.0 / (1.0 + decay_rate + spread_rate * stiffness)
        coarse = 1.0 / (1.0 + M * decay_rate + M * spread_rate * stiffness)
        fine = fine_factor
        symbol = fine
        for _ in range(M - 1):
            fine = fine * fine_factor
            symbol = symbol + fine

        def slot(turn):
            return pl.ds(pl.multiple_of(turn * width + row, 8), 8)

        initial = scale * spectra[slot(turns - 2), lane]
        forcing = symbol * (scale * spectra[slot(turns - 1), lane])
        state = fine * initial + forcing
        states[slot(0), lane] = state
        state = fine * state + forcing
        states[slot(1), lane] = state
        gain = (fine * scale) * (fine - coarse)
        source_gain = (1.0 + fine - coarse) * forcing
        for turn in range(2, turns):
            state = coarse * state + (gain * spectra[slot(turn - 2), lane] + source_gain)
            states[slot(turn), lane] = state
        return carry

    lax.fori_loop(0, width // 8 * (length // lanes), mix, 0)

    part = batch // 2
    for turn in range(2):
        which = lax.rem(my_half + 1 + turn, 2)
        block = pl.ds(pl.multiple_of(which * part, part), part)
        even_high, even_low = split(states[block, :half])
        odd_high, odd_low = split(states[block, half:])
        for shard in range(shards // 2):
            columns = slice(shard * rows, (shard + 1) * rows)
            even = dot3(even_high, even_low, kernels[0, 0, :, columns], kernels[1, 0, :, columns])
            odd = dot3(odd_high, odd_low, kernels[0, 1, :, columns], kernels[1, 1, :, columns])
            spread[shard, block, :] = even + odd
            spread[shard + shards // 2, block, :] = even - odd
        send_half(which, second_copy)

    own = pltpu.make_async_copy(
        spread.at[space, pl.ds(pl.multiple_of(tm * width, width), width), :],
        returned.at[pl.ds(pl.multiple_of(me * width, width), width), :], own_sem.at[1])
    own.start()
    own.wait()

    def arrive_two(step, carry):
        peer = lax.rem(me + step, devices)
        pltpu.make_async_remote_copy(
            src_ref=spread.at[0, pl.ds(0, width), :],
            dst_ref=returned.at[pl.ds(pl.multiple_of(peer * width, width), width), :],
            send_sem=send_two.at[peer], recv_sem=recv_two.at[peer],
            device_id=(peer // shards, lax.rem(peer, shards)), device_id_type=MESH).wait_recv()
        return carry

    lax.fori_loop(1, devices, arrive_two, 0)

    even_high, even_low = split(returned[:half, :].T)
    odd_high, odd_low = split(returned[half:, :].T)
    for index in range(half // tile):
        columns = slice(index * tile, (index + 1) * tile)
        even = dot3(even_high, even_low, kernels[0, 0, :, columns], kernels[1, 0, :, columns])
        odd = dot3(odd_high, odd_low, kernels[0, 1, :, columns], kernels[1, 1, :, columns])
        out_ref[0, :, index * tile:(index + 1) * tile] = even + odd
        out_ref[0, :, half + index * tile:half + (index + 1) * tile] = even - odd

    def sent(step, carry):
        peer = lax.rem(me + step, devices)
        first_copy(peer).wait_send()
        second_copy(peer).wait_send()
        return carry

    lax.fori_loop(1, devices, sent, 0)


def body(turns, shards, initial_guess, start_field, source_field):
    rows, length = start_field.shape
    devices = turns * shards
    half, width = length // 2, length // devices
    batch = turns * width
    kernels = jnp.asarray(half_kernels(length))
    sines = (np.sin(np.pi * mode_order(length) / length) ** 2).astype(np.float32)
    row_sines = jnp.asarray(np.repeat(sines[:, None], 128, axis=1))
    column_sines = jnp.asarray(np.repeat(sines[None, :], 8, axis=0))
    tall = max(rows, batch)
    dma = pltpu.SemaphoreType.DMA
    anywhere = pl.BlockSpec(memory_space=pl.ANY)
    local = pl.BlockSpec(memory_space=pltpu.VMEM)
    return pl.pallas_call(
        functools.partial(mgrit_kernel, turns, shards),
        out_shape=jax.ShapeDtypeStruct(initial_guess.shape, jnp.float32),
        in_specs=[anywhere] * 5 + [local],
        out_specs=local,
        scratch_shapes=[
            pltpu.VMEM((rows, length), jnp.float32),
            pltpu.VMEM((2, 2, half, half), jnp.bfloat16),
            pltpu.VMEM((width, 128), jnp.float32),
            pltpu.VMEM((2, tall, half), jnp.bfloat16),
            pltpu.VMEM((2, tall, half), jnp.bfloat16),
            pltpu.VMEM((length, rows), jnp.float32),
            pltpu.VMEM((shards, batch, rows), jnp.float32),
            pltpu.VMEM((batch, length), jnp.float32),
            pltpu.VMEM((batch, length), jnp.float32),
            pltpu.VMEM((shards, batch, rows), jnp.float32),
            pltpu.VMEM((length, rows), jnp.float32),
            dma, dma, dma, dma((devices,)), dma((devices,)), dma((devices,)), dma((devices,)), dma((2,)),
        ],
        compiler_params=pltpu.CompilerParams(
            collective_id=0, has_side_effects=True, vmem_limit_bytes=32 * 1024 * 1024),
    )(initial_guess, start_field, source_field, kernels, row_sines, column_sines)


def solution(mesh):
    return jax.shard_map(
        functools.partial(body, mesh.shape["tm"], mesh.shape["space"]),
        mesh=mesh,
        in_specs=(P("tm", "space", None), P("space", None), P("space", None)),
        out_specs=P("tm", "space", None),
        check_vma=False,
    )
```

```python
import functools

import jax
import jax.numpy as jnp
import numpy as np
from jax import lax
from jax.experimental import pallas as pl
from jax.experimental.pallas import tpu as pltpu
from jax.sharding import PartitionSpec as P

M = 16
MESH = pl.DeviceIdType.MESH

decay_rate = 0.0005
spread_rate = 0.01


def mode_order(length):
    return np.concatenate([np.arange(0, length, 2), np.arange(1, length, 2)])


def half_kernels(length):
    half = length // 2
    product = mode_order(length)[:, None] * np.arange(half)[None, :] % length
    angles = 2.0 * np.pi / length * product
    full = (np.cos(angles) + np.sin(angles)).astype(np.float32).reshape(2, half, half)
    high = full.astype(jnp.bfloat16)
    low = (full - high.astype(np.float32)).astype(jnp.bfloat16)
    return np.stack([high, low])


def split(value):
    high = value.astype(jnp.bfloat16)
    low = (value - high.astype(jnp.float32)).astype(jnp.bfloat16)
    return high, low


def dot(a, b, transposed):
    dims = (((1,), (1 if transposed else 0,)), ((), ()))
    return lax.dot_general(a, b, dims, preferred_element_type=jnp.float32)


def dot3(a_high, a_low, b_high, b_low, transposed=False):
    return (
        dot(a_high, b_high, transposed)
        + (dot(a_low, b_high, transposed) + dot(a_high, b_low, transposed))
    )


def mgrit_kernel(
    turns, shards, chunks,
    guess, start, source, kernels_hbm, rows_hbm, columns_hbm, out_ref,
    field, kernels, row_sines, column_sines, sums_high, sums_low, along, gathered, spectra, states, spread, returned,
    load_sem, kernel_sem, rows_sem, columns_sem, send_one, recv_one, send_two, recv_two, own_sem,
):
    tm, space = lax.axis_index("tm"), lax.axis_index("space")
    devices = turns * shards
    me = tm * shards + space
    group = devices // 2
    my_half = me // group
    rows, length = field.shape
    half = length // 2
    width = length // devices

    kernel_load = pltpu.make_async_copy(kernels_hbm, kernels, kernel_sem)
    kernel_load.start()
    rows_load = pltpu.make_async_copy(
        rows_hbm.at[pl.ds(pl.multiple_of(me * width, width), width), :], row_sines, rows_sem)
    rows_load.start()
    columns_load = pltpu.make_async_copy(columns_hbm, column_sines, columns_sem)
    columns_load.start()

    barrier = pltpu.get_barrier_semaphore()

    def greet(step, carry):
        peer = lax.rem(me + step, devices)
        pl.semaphore_signal(barrier, inc=1, device_id=(peer // shards, lax.rem(peer, shards)), device_id_type=MESH)
        return carry

    lax.fori_loop(1, devices, greet, 0)

    @pl.when(tm < turns - 2)
    def _():
        load = pltpu.make_async_copy(guess.at[0], field, load_sem)
        load.start()
        load.wait()

    @pl.when(tm == turns - 2)
    def _():
        load = pltpu.make_async_copy(start, field, load_sem)
        load.start()
        load.wait()

    @pl.when(tm == turns - 1)
    def _():
        load = pltpu.make_async_copy(source, field, load_sem)
        load.start()
        load.wait()

    first, second = field[:, :half], field[:, half:]
    sums_high[0, :rows], sums_low[0, :rows] = split(first + second)
    sums_high[1, :rows], sums_low[1, :rows] = split(first - second)
    kernel_load.wait()

    def first_copy(peer):
        return pltpu.make_async_remote_copy(
            src_ref=along.at[pl.ds(pl.multiple_of(peer * width, width), width), :],
            dst_ref=gathered.at[space, pl.ds(pl.multiple_of(tm * width, width), width), :],
            send_sem=send_one.at[peer], recv_sem=recv_one.at[me],
            device_id=(peer // shards, lax.rem(peer, shards)), device_id_type=MESH)

    def second_copy(peer, chunk):
        turn, shard = peer // shards, lax.rem(peer, shards)
        return pltpu.make_async_remote_copy(
            src_ref=spread.at[shard, pl.ds(pl.multiple_of(chunk * chunk_rows + turn * deep, deep), deep), :],
            dst_ref=returned.at[pl.ds(pl.multiple_of(me * width + chunk * deep, deep), deep), :],
            send_sem=send_two.at[chunk, peer], recv_sem=recv_two.at[chunk, me],
            device_id=(turn, shard), device_id_type=MESH)

    def send_range(lowest, count, copy_to):
        def send(step, carry):
            peer = lowest + lax.rem(me + step, count)

            @pl.when(peer != me)
            def _():
                copy_to(peer).start()

            return carry

        lax.fori_loop(0, count, send, 0)

    def arrive(which, copy_from):
        def wait(step, carry):
            peer = which * group + lax.rem(me + step, group)

            @pl.when(peer != me)
            def _():
                copy_from(peer).wait_recv()

            return carry

        lax.fori_loop(0, group, wait, 0)

    batch = turns * width
    part = batch // 2
    deep = width // chunks
    chunk_rows = turns * deep
    chunk_part = chunk_rows // 2
    tile = min(half, 256)
    plane = tile // width

    pl.semaphore_wait(barrier, devices - 1)
    for turn in range(2):
        which = lax.rem(my_half + 1 + turn, 2)

        def row_tile(index, carry, which=which):
            offset = pl.multiple_of(index * tile, tile)
            result = dot3(
                kernels[0, which, pl.ds(offset, tile), :], kernels[1, which, pl.ds(offset, tile), :],
                sums_high[which, :rows], sums_low[which, :rows], True)
            along[pl.ds(pl.multiple_of(which * half + index * tile, tile), tile), :] = result
            send_range(which * group + index * plane, plane, first_copy)
            return carry

        lax.fori_loop(0, half // tile, row_tile, 0)

    own = pltpu.make_async_copy(
        along.at[pl.ds(pl.multiple_of(me * width, width), width), :],
        gathered.at[space, pl.ds(pl.multiple_of(tm * width, width), width), :], own_sem.at[0])
    own.start()
    own.wait()
    rows_load.wait()
    columns_load.wait()

    def first_from(peer):
        return pltpu.make_async_remote_copy(
            src_ref=along.at[pl.ds(pl.multiple_of(me * width, width), width), :],
            dst_ref=gathered.at[lax.rem(peer, shards), pl.ds(pl.multiple_of(peer // shards * width, width), width), :],
            send_sem=send_one.at[peer], recv_sem=recv_one.at[peer],
            device_id=(peer // shards, lax.rem(peer, shards)), device_id_type=MESH)

    for turn in range(2):
        side = lax.rem(my_half + turn, 2)
        arrive(side, first_from)
        block = pl.ds(pl.multiple_of(side * part, part), part)
        for shard in range(shards // 2):
            columns = slice(shard * rows, (shard + 1) * rows)
            upper, lower = gathered[shard, block, :], gathered[shard + shards // 2, block, :]
            sums_high[0, :part, columns], sums_low[0, :part, columns] = split(upper + lower)
            sums_high[1, :part, columns], sums_low[1, :part, columns] = split(upper - lower)
        for which in range(2):
            def column_tile(index, carry, which=which, block=block):
                offset = pl.multiple_of(index * tile, tile)
                spectra[block, pl.ds(pl.multiple_of(which * half + index * tile, tile), tile)] = dot3(
                    sums_high[which, :part], sums_low[which, :part],
                    kernels[0, which, pl.ds(offset, tile), :], kernels[1, which, pl.ds(offset, tile), :], True)
                return carry

            lax.fori_loop(0, half // tile, column_tile, 0)

    lanes = 256
    scale = 1.0 / float(length * length)

    def mix(chunk, index, carry):
        row = pl.multiple_of(index // (length // lanes) * 8, 8)
        lane = pl.ds(pl.multiple_of(lax.rem(index, length // lanes) * lanes, lanes), lanes)
        row_part = jnp.concatenate([row_sines[pl.ds(chunk * deep + row, 8), :]] * (lanes // 128), axis=1)
        stiffness = 4.0 * (column_sines[:, lane] + row_part)
        fine_factor = 1.0 / (1.0 + decay_rate + spread_rate * stiffness)
        coarse = 1.0 / (1.0 + M * decay_rate + M * spread_rate * stiffness)
        fine = fine_factor
        symbol = fine
        for _ in range(M - 1):
            fine = fine * fine_factor
            symbol = symbol + fine

        def read(turn):
            return spectra[pl.ds(pl.multiple_of(turn * width + chunk * deep + row, 8), 8), lane]

        def write(turn, value):
            states[pl.ds(pl.multiple_of(chunk * chunk_rows + turn * deep + row, 8), 8), lane] = value

        initial = scale * read(turns - 2)
        forcing = symbol * (scale * read(turns - 1))
        state = fine * initial + forcing
        write(0, state)
        state = fine * state + forcing
        write(1, state)
        gain = (fine * scale) * (fine - coarse)
        source_gain = (1.0 + fine - coarse) * forcing
        for turn in range(2, turns):
            state = coarse * state + (gain * read(turn - 2) + source_gain)
            write(turn, state)
        return carry

    def undo_columns(chunk, which):
        block = pl.ds(pl.multiple_of(chunk * chunk_rows + which * chunk_part, chunk_part), chunk_part)
        even_high, even_low = split(states[block, :half])
        odd_high, odd_low = split(states[block, half:])
        for shard in range(shards // 2):
            columns = slice(shard * rows, (shard + 1) * rows)
            even = dot3(even_high, even_low, kernels[0, 0, :, columns], kernels[1, 0, :, columns])
            odd = dot3(odd_high, odd_low, kernels[0, 1, :, columns], kernels[1, 1, :, columns])
            spread[shard, block, :] = even + odd
            spread[shard + shards // 2, block, :] = even - odd
        send_range(which * group, group, functools.partial(second_copy, chunk=chunk))

    for chunk in range(chunks):
        lax.fori_loop(0, deep // 8 * (length // lanes), functools.partial(mix, chunk), 0)
        undo_columns(chunk, 1 - my_half)
    for chunk in range(chunks):
        undo_columns(chunk, my_half)

    for chunk in range(chunks):
        own = pltpu.make_async_copy(
            spread.at[space, pl.ds(pl.multiple_of(chunk * chunk_rows + tm * deep, deep), deep), :],
            returned.at[pl.ds(pl.multiple_of(me * width + chunk * deep, deep), deep), :], own_sem.at[1 + chunk])
        own.start()
        own.wait()

    def second_from(peer, chunk):
        return pltpu.make_async_remote_copy(
            src_ref=spread.at[0, pl.ds(0, deep), :],
            dst_ref=returned.at[pl.ds(pl.multiple_of(peer * width + chunk * deep, deep), deep), :],
            send_sem=send_two.at[chunk, peer], recv_sem=recv_two.at[chunk, peer],
            device_id=(peer // shards, lax.rem(peer, shards)), device_id_type=MESH)

    def undo_rows(which):
        for chunk in range(chunks):
            arrive(which, functools.partial(second_from, chunk=chunk))
        high, low = split(returned[pl.ds(pl.multiple_of(which * half, half), half), :].T)
        return [
            dot3(high, low, kernels[0, which, :, columns], kernels[1, which, :, columns])
            for columns in (slice(index, index + tile) for index in range(0, half, tile))
        ]

    for index, near in enumerate(undo_rows(my_half)):
        field[:, index * tile:(index + 1) * tile] = near
    sign = 1.0 - 2.0 * my_half.astype(jnp.float32)
    for index, far in enumerate(undo_rows(1 - my_half)):
        near = field[:, index * tile:(index + 1) * tile]
        out_ref[0, :, index * tile:(index + 1) * tile] = near + far
        out_ref[0, :, half + index * tile:half + (index + 1) * tile] = sign * (near - far)

    def sent(step, carry):
        peer = lax.rem(me + step, devices)
        first_copy(peer).wait_send()
        for chunk in range(chunks):
            second_copy(peer, chunk).wait_send()
        return carry

    lax.fori_loop(1, devices, sent, 0)


def body(turns, shards, initial_guess, start_field, source_field):
    rows, length = start_field.shape
    devices = turns * shards
    half, width = length // 2, length // devices
    batch = turns * width
    kernels = jnp.asarray(half_kernels(length))
    sines = (np.sin(np.pi * mode_order(length) / length) ** 2).astype(np.float32)
    row_sines = jnp.asarray(np.repeat(sines[:, None], 128, axis=1))
    column_sines = jnp.asarray(np.repeat(sines[None, :], 8, axis=0))
    chunks = 2 if width % 16 == 0 else 1
    tall = max(rows, batch)
    dma = pltpu.SemaphoreType.DMA
    anywhere = pl.BlockSpec(memory_space=pltpu.HBM)
    local = pl.BlockSpec(memory_space=pltpu.VMEM)
    return pl.pallas_call(
        functools.partial(mgrit_kernel, turns, shards, chunks),
        out_shape=jax.ShapeDtypeStruct(initial_guess.shape, jnp.float32),
        in_specs=[anywhere] * 6,
        out_specs=local,
        scratch_shapes=[
            pltpu.VMEM((rows, length), jnp.float32),
            pltpu.VMEM((2, 2, half, half), jnp.bfloat16),
            pltpu.VMEM((width, 128), jnp.float32),
            pltpu.VMEM((8, length), jnp.float32),
            pltpu.VMEM((2, tall, half), jnp.bfloat16),
            pltpu.VMEM((2, tall, half), jnp.bfloat16),
            pltpu.VMEM((length, rows), jnp.float32),
            pltpu.VMEM((shards, batch, rows), jnp.float32),
            pltpu.VMEM((batch, length), jnp.float32),
            pltpu.VMEM((batch, length), jnp.float32),
            pltpu.VMEM((shards, batch, rows), jnp.float32),
            pltpu.VMEM((length, rows), jnp.float32),
            dma, dma, dma, dma, dma((devices,)), dma((devices,)),
            dma((chunks, devices)), dma((chunks, devices)), dma((1 + chunks,)),
        ],
        compiler_params=pltpu.CompilerParams(
            collective_id=0, has_side_effects=True, vmem_limit_bytes=60 * 1024 * 1024),
    )(initial_guess, start_field, source_field, kernels, row_sines, column_sines)


def solution(mesh):
    return jax.shard_map(
        functools.partial(body, mesh.shape["tm"], mesh.shape["space"]),
        mesh=mesh,
        in_specs=(P("tm", "space", None), P("space", None), P("space", None)),
        out_specs=P("tm", "space", None),
        check_vma=False,
    )
```

```python
import functools

import jax
import jax.numpy as jnp
import numpy as np
from jax import lax
from jax.experimental import pallas as pl
from jax.experimental.pallas import tpu as pltpu
from jax.sharding import PartitionSpec as P

M = 16
MESH = pl.DeviceIdType.MESH

decay_rate = 0.0005
spread_rate = 0.01


def mode_order(length):
    return np.concatenate([np.arange(0, length, 2), np.arange(1, length, 2)])


def half_kernels(length):
    half = length // 2
    product = mode_order(length)[:, None] * np.arange(half)[None, :] % length
    angles = 2.0 * np.pi / length * product
    full = (np.cos(angles) + np.sin(angles)).astype(np.float32).reshape(2, half, half)
    high = full.astype(jnp.bfloat16)
    low = (full - high.astype(np.float32)).astype(jnp.bfloat16)
    return np.stack([high, low])


def split(value):
    high = value.astype(jnp.bfloat16)
    low = (value - high.astype(jnp.float32)).astype(jnp.bfloat16)
    return high, low


def dot(a, b, transposed):
    dims = (((1,), (1 if transposed else 0,)), ((), ()))
    return lax.dot_general(a, b, dims, preferred_element_type=jnp.float32)


def dot3(a_high, a_low, b_high, b_low, transposed=False):
    return (
        dot(a_high, b_high, transposed)
        + (dot(a_low, b_high, transposed) + dot(a_high, b_low, transposed))
    )


def mgrit_kernel(
    turns, shards, chunks,
    guess, start, source, kernels_hbm, rows_hbm, columns_hbm, out_ref,
    field, kernels, row_sines, column_sines, sums_high, sums_low, along, gathered, spectra, states, spread, returned,
    load_sem, kernel_sem, rows_sem, columns_sem, send_one, recv_one, send_two, recv_two, own_sem,
):
    tm, space = lax.axis_index("tm"), lax.axis_index("space")
    devices = turns * shards
    me = tm * shards + space
    group = devices // 2
    my_half = me // group
    rows, length = field.shape
    half = length // 2
    width = length // devices

    kernel_load = pltpu.make_async_copy(kernels_hbm, kernels, kernel_sem)
    kernel_load.start()
    rows_load = pltpu.make_async_copy(
        rows_hbm.at[pl.ds(pl.multiple_of(me * width, width), width), :], row_sines, rows_sem)
    rows_load.start()
    columns_load = pltpu.make_async_copy(columns_hbm, column_sines, columns_sem)
    columns_load.start()

    barrier = pltpu.get_barrier_semaphore()

    def greet(step, carry):
        peer = lax.rem(me + step, devices)
        pl.semaphore_signal(barrier, inc=1, device_id=(peer // shards, lax.rem(peer, shards)), device_id_type=MESH)
        return carry

    lax.fori_loop(1, devices, greet, 0)

    @pl.when(tm < turns - 2)
    def _():
        load = pltpu.make_async_copy(guess.at[0], field, load_sem)
        load.start()
        load.wait()

    @pl.when(tm == turns - 2)
    def _():
        load = pltpu.make_async_copy(start, field, load_sem)
        load.start()
        load.wait()

    @pl.when(tm == turns - 1)
    def _():
        load = pltpu.make_async_copy(source, field, load_sem)
        load.start()
        load.wait()

    first, second = field[:, :half], field[:, half:]
    sums_high[0, :rows], sums_low[0, :rows] = split(first + second)
    sums_high[1, :rows], sums_low[1, :rows] = split(first - second)
    kernel_load.wait()

    def first_copy(peer):
        return pltpu.make_async_remote_copy(
            src_ref=along.at[pl.ds(pl.multiple_of(peer * width, width), width), :],
            dst_ref=gathered.at[space, pl.ds(pl.multiple_of(tm * width, width), width), :],
            send_sem=send_one.at[peer], recv_sem=recv_one.at[me],
            device_id=(peer // shards, lax.rem(peer, shards)), device_id_type=MESH)

    def second_copy(peer, chunk):
        turn, shard = peer // shards, lax.rem(peer, shards)
        return pltpu.make_async_remote_copy(
            src_ref=spread.at[shard, pl.ds(pl.multiple_of(chunk * chunk_rows + turn * deep, deep), deep), :],
            dst_ref=returned.at[pl.ds(pl.multiple_of(me * width + chunk * deep, deep), deep), :],
            send_sem=send_two.at[chunk, peer], recv_sem=recv_two.at[chunk, me],
            device_id=(turn, shard), device_id_type=MESH)

    def send_range(lowest, count, copy_to):
        def send(step, carry):
            peer = lowest + lax.rem(me + step, count)

            @pl.when(peer != me)
            def _():
                copy_to(peer).start()

            return carry

        lax.fori_loop(0, count, send, 0)

    def arrive(which, copy_from):
        def wait(step, carry):
            peer = which * group + lax.rem(me + step, group)

            @pl.when(peer != me)
            def _():
                copy_from(peer).wait_recv()

            return carry

        lax.fori_loop(0, group, wait, 0)

    batch = turns * width
    part = batch // 2
    deep = width // chunks
    chunk_rows = turns * deep
    chunk_part = chunk_rows // 2
    tile = min(half, 256)
    plane = tile // width

    pl.semaphore_wait(barrier, devices - 1)
    for turn in range(2):
        which = lax.rem(my_half + 1 + turn, 2)

        def row_tile(index, carry, which=which):
            offset = pl.multiple_of(index * tile, tile)
            result = dot3(
                kernels[0, which, pl.ds(offset, tile), :], kernels[1, which, pl.ds(offset, tile), :],
                sums_high[which, :rows], sums_low[which, :rows], True)
            along[pl.ds(pl.multiple_of(which * half + index * tile, tile), tile), :] = result
            send_range(which * group + index * plane, plane, first_copy)
            return carry

        lax.fori_loop(0, half // tile, row_tile, 0)

    own = pltpu.make_async_copy(
        along.at[pl.ds(pl.multiple_of(me * width, width), width), :],
        gathered.at[space, pl.ds(pl.multiple_of(tm * width, width), width), :], own_sem.at[0])
    own.start()
    own.wait()
    rows_load.wait()
    columns_load.wait()

    def first_from(peer):
        return pltpu.make_async_remote_copy(
            src_ref=along.at[pl.ds(pl.multiple_of(me * width, width), width), :],
            dst_ref=gathered.at[lax.rem(peer, shards), pl.ds(pl.multiple_of(peer // shards * width, width), width), :],
            send_sem=send_one.at[peer], recv_sem=recv_one.at[peer],
            device_id=(peer // shards, lax.rem(peer, shards)), device_id_type=MESH)

    for turn in range(2):
        side = lax.rem(my_half + turn, 2)
        arrive(side, first_from)
        block = pl.ds(pl.multiple_of(side * part, part), part)
        for shard in range(shards // 2):
            columns = slice(shard * rows, (shard + 1) * rows)
            upper, lower = gathered[shard, block, :], gathered[shard + shards // 2, block, :]
            sums_high[0, :part, columns], sums_low[0, :part, columns] = split(upper + lower)
            sums_high[1, :part, columns], sums_low[1, :part, columns] = split(upper - lower)
        for which in range(2):
            def column_tile(index, carry, which=which, block=block):
                offset = pl.multiple_of(index * tile, tile)
                spectra[block, pl.ds(pl.multiple_of(which * half + index * tile, tile), tile)] = dot3(
                    sums_high[which, :part], sums_low[which, :part],
                    kernels[0, which, pl.ds(offset, tile), :], kernels[1, which, pl.ds(offset, tile), :], True)
                return carry

            lax.fori_loop(0, half // tile, column_tile, 0)

    lanes = 256
    scale = 1.0 / float(length * length)

    def mix(chunk, index, carry):
        row = pl.multiple_of(index // (length // lanes) * 8, 8)
        lane = pl.ds(pl.multiple_of(lax.rem(index, length // lanes) * lanes, lanes), lanes)
        row_part = jnp.concatenate([row_sines[pl.ds(chunk * deep + row, 8), :]] * (lanes // 128), axis=1)
        stiffness = 4.0 * (column_sines[:, lane] + row_part)
        fine_factor = 1.0 / (1.0 + decay_rate + spread_rate * stiffness)
        coarse = 1.0 / (1.0 + M * decay_rate + M * spread_rate * stiffness)
        fine = fine_factor
        symbol = fine
        for _ in range(M - 1):
            fine = fine * fine_factor
            symbol = symbol + fine

        def read(turn):
            return spectra[pl.ds(pl.multiple_of(turn * width + chunk * deep + row, 8), 8), lane]

        def write(turn, value):
            states[pl.ds(pl.multiple_of(chunk * chunk_rows + turn * deep + row, 8), 8), lane] = value

        initial = scale * read(turns - 2)
        forcing = symbol * (scale * read(turns - 1))
        state = fine * initial + forcing
        write(0, state)
        state = fine * state + forcing
        write(1, state)
        gain = (fine * scale) * (fine - coarse)
        source_gain = (1.0 + fine - coarse) * forcing
        for turn in range(2, turns):
            state = coarse * state + (gain * read(turn - 2) + source_gain)
            write(turn, state)
        return carry

    def undo_columns(chunk, which):
        block = pl.ds(pl.multiple_of(chunk * chunk_rows + which * chunk_part, chunk_part), chunk_part)
        even_high, even_low = split(states[block, :half])
        odd_high, odd_low = split(states[block, half:])
        for shard in range(shards // 2):
            columns = slice(shard * rows, (shard + 1) * rows)
            even = dot3(even_high, even_low, kernels[0, 0, :, columns], kernels[1, 0, :, columns])
            odd = dot3(odd_high, odd_low, kernels[0, 1, :, columns], kernels[1, 1, :, columns])
            spread[shard, block, :] = even + odd
            spread[shard + shards // 2, block, :] = even - odd
        send_range(which * group, group, functools.partial(second_copy, chunk=chunk))

    for chunk in range(chunks):
        lax.fori_loop(0, deep // 8 * (length // lanes), functools.partial(mix, chunk), 0)
        undo_columns(chunk, 1 - my_half)
    for chunk in range(chunks):
        undo_columns(chunk, my_half)

    for chunk in range(chunks):
        own = pltpu.make_async_copy(
            spread.at[space, pl.ds(pl.multiple_of(chunk * chunk_rows + tm * deep, deep), deep), :],
            returned.at[pl.ds(pl.multiple_of(me * width + chunk * deep, deep), deep), :], own_sem.at[1 + chunk])
        own.start()
        own.wait()

    def second_from(peer, chunk):
        return pltpu.make_async_remote_copy(
            src_ref=spread.at[0, pl.ds(0, deep), :],
            dst_ref=returned.at[pl.ds(pl.multiple_of(peer * width + chunk * deep, deep), deep), :],
            send_sem=send_two.at[chunk, peer], recv_sem=recv_two.at[chunk, peer],
            device_id=(peer // shards, lax.rem(peer, shards)), device_id_type=MESH)

    def undo_rows(which):
        for chunk in range(chunks):
            arrive(which, functools.partial(second_from, chunk=chunk))
        high, low = split(returned[pl.ds(pl.multiple_of(which * half, half), half), :].T)
        return [
            dot3(high, low, kernels[0, which, :, columns], kernels[1, which, :, columns])
            for columns in (slice(index, index + tile) for index in range(0, half, tile))
        ]

    for index, near in enumerate(undo_rows(my_half)):
        field[:, index * tile:(index + 1) * tile] = near
    sign = 1.0 - 2.0 * my_half.astype(jnp.float32)
    for index, far in enumerate(undo_rows(1 - my_half)):
        near = field[:, index * tile:(index + 1) * tile]
        out_ref[0, :, index * tile:(index + 1) * tile] = near + far
        out_ref[0, :, half + index * tile:half + (index + 1) * tile] = sign * (near - far)

    def sent(step, carry):
        peer = lax.rem(me + step, devices)
        first_copy(peer).wait_send()
        for chunk in range(chunks):
            second_copy(peer, chunk).wait_send()
        return carry

    lax.fori_loop(1, devices, sent, 0)


def body(turns, shards, initial_guess, start_field, source_field):
    rows, length = start_field.shape
    devices = turns * shards
    half, width = length // 2, length // devices
    batch = turns * width
    kernels = jnp.asarray(half_kernels(length))
    sines = (np.sin(np.pi * mode_order(length) / length) ** 2).astype(np.float32)
    row_sines = jnp.asarray(np.repeat(sines[:, None], 128, axis=1))
    column_sines = jnp.asarray(np.repeat(sines[None, :], 8, axis=0))
    chunks = 2 if width % 16 == 0 else 1
    tall = max(rows, batch)
    dma = pltpu.SemaphoreType.DMA
    anywhere = pl.BlockSpec(memory_space=pltpu.HBM)
    local = pl.BlockSpec(memory_space=pltpu.VMEM)
    return pl.pallas_call(
        functools.partial(mgrit_kernel, turns, shards, chunks),
        out_shape=jax.ShapeDtypeStruct(initial_guess.shape, jnp.float32),
        in_specs=[anywhere] * 6,
        out_specs=local,
        scratch_shapes=[
            pltpu.VMEM((rows, length), jnp.float32),
            pltpu.VMEM((2, 2, half, half), jnp.bfloat16),
            pltpu.VMEM((width, 128), jnp.float32),
            pltpu.VMEM((8, length), jnp.float32),
            pltpu.VMEM((2, tall, half), jnp.bfloat16),
            pltpu.VMEM((2, tall, half), jnp.bfloat16),
            pltpu.VMEM((length, rows), jnp.float32),
            pltpu.VMEM((shards, batch, rows), jnp.float32),
            pltpu.VMEM((batch, length), jnp.float32),
            pltpu.VMEM((batch, length), jnp.float32),
            pltpu.VMEM((shards, batch, rows), jnp.float32),
            pltpu.VMEM((length, rows), jnp.float32),
            dma, dma, dma, dma, dma((devices,)), dma((devices,)),
            dma((chunks, devices)), dma((chunks, devices)), dma((1 + chunks,)),
        ],
        compiler_params=pltpu.CompilerParams(
            collective_id=0, has_side_effects=True, vmem_limit_bytes=32 * 1024 * 1024),
    )(*(pltpu.with_memory_space_constraint(value, pltpu.HBM)
        for value in (initial_guess, start_field, source_field, kernels, row_sines, column_sines)))


def solution(mesh):
    return jax.shard_map(
        functools.partial(body, mesh.shape["tm"], mesh.shape["space"]),
        mesh=mesh,
        in_specs=(P("tm", "space", None), P("space", None), P("space", None)),
        out_specs=P("tm", "space", None),
        check_vma=False,
    )
```

```python
import functools

import jax
import jax.numpy as jnp
import numpy as np
from jax import lax
from jax.experimental import pallas as pl
from jax.experimental.pallas import tpu as pltpu
from jax.sharding import PartitionSpec as P

M = 16
MESH = pl.DeviceIdType.MESH

decay_rate = 0.0005
spread_rate = 0.01


def mode_order(length):
    return np.concatenate([np.arange(0, length, 2), np.arange(1, length, 2)])


def half_kernels(length):
    half = length // 2
    product = mode_order(length)[:, None] * np.arange(half)[None, :] % length
    angles = 2.0 * np.pi / length * product
    full = (np.cos(angles) + np.sin(angles)).astype(np.float32).reshape(2, half, half)
    high = full.astype(jnp.bfloat16)
    low = (full - high.astype(np.float32)).astype(jnp.bfloat16)
    return np.stack([high, low])


def split(value):
    high = value.astype(jnp.bfloat16)
    low = (value - high.astype(jnp.float32)).astype(jnp.bfloat16)
    return high, low


def dot(a, b, transposed):
    dims = (((1,), (1 if transposed else 0,)), ((), ()))
    return lax.dot_general(a, b, dims, preferred_element_type=jnp.float32)


def dot3(a_high, a_low, b_high, b_low, transposed=False):
    return (
        dot(a_high, b_high, transposed)
        + (dot(a_low, b_high, transposed) + dot(a_high, b_low, transposed))
    )


def mgrit_kernel(
    turns, shards, chunks,
    guess, start, source, kernels_hbm, rows_hbm, columns_hbm, out_ref,
    field, extra, kernels, row_sines, column_sines, field_high, field_low, extra_high, extra_low,
    sums_high, sums_low, along, along_extra, gathered, gathered_extra, spectra, states, crossing, incoming,
    spread, returned,
    load_sem, kernel_sem, rows_sem, columns_sem, send_one, recv_one, send_extra, recv_extra,
    send_cross, recv_cross, send_two, recv_two, own_sem,
):
    tm, space = lax.axis_index("tm"), lax.axis_index("space")
    devices = turns * shards
    group = devices // 2
    turns_here = turns // 2
    side = tm // turns_here
    place = lax.rem(tm, turns_here)
    me = place * shards + space
    rows, length = field.shape
    half = length // 2
    tile = length // chunks
    deep = tile // group
    slots = turns_here * deep
    per_parity = chunks // 2
    has_guess = tm < turns - 2

    field_load = pltpu.make_async_copy(guess.at[0], field, load_sem.at[0])
    field_load.start()
    kernel_load = pltpu.make_async_copy(kernels_hbm, kernels, kernel_sem)
    kernel_load.start()
    start_load = pltpu.make_async_copy(start, extra.at[pl.ds(0, rows), :], load_sem.at[1])
    start_load.start()
    source_load = pltpu.make_async_copy(source, extra.at[pl.ds(rows, rows), :], load_sem.at[2])
    source_load.start()
    rows_loads = []
    for chunk in range(chunks):
        load = pltpu.make_async_copy(
            rows_hbm.at[pl.ds(pl.multiple_of(chunk * tile + me * deep, deep), deep), :],
            row_sines.at[pl.ds(chunk * deep, deep), :], rows_sem.at[chunk])
        load.start()
        rows_loads.append(load)
    columns_load = pltpu.make_async_copy(columns_hbm, column_sines, columns_sem)
    columns_load.start()

    def device(peer):
        return (side * turns_here + peer // shards, lax.rem(peer, shards))

    other = (lax.rem(tm + turns_here, turns), space)
    barrier = pltpu.get_barrier_semaphore()

    def greet(step, carry):
        pl.semaphore_signal(barrier, inc=1, device_id=device(lax.rem(me + step, group)), device_id_type=MESH)
        return carry

    lax.fori_loop(1, group, greet, 0)
    pl.semaphore_signal(barrier, inc=1, device_id=other, device_id_type=MESH)

    def rows_of(base, index):
        return pl.ds(pl.multiple_of(base + index * deep, deep), deep)

    def first_copy(chunk, peer, origin=None):
        origin = me if origin is None else origin
        return pltpu.make_async_remote_copy(
            src_ref=along.at[rows_of(chunk * tile, peer), :],
            dst_ref=gathered.at[chunk, lax.rem(origin, shards), rows_of(0, origin // shards), :],
            send_sem=send_one.at[chunk, peer], recv_sem=recv_one.at[chunk, origin],
            device_id=device(peer), device_id_type=MESH)

    def extra_copy(chunk, shard, origin=None):
        origin = space if origin is None else origin
        return pltpu.make_async_remote_copy(
            src_ref=along_extra.at[chunk, rows_of(0, shard), :],
            dst_ref=gathered_extra.at[chunk, origin],
            send_sem=send_extra.at[chunk, shard], recv_sem=recv_extra.at[chunk, origin],
            device_id=(tm, shard), device_id_type=MESH)

    def cross_copy(chunk):
        return pltpu.make_async_remote_copy(
            src_ref=crossing.at[chunk], dst_ref=incoming.at[chunk],
            send_sem=send_cross.at[chunk], recv_sem=recv_cross.at[chunk],
            device_id=other, device_id_type=MESH)

    def second_copy(chunk, peer, origin=None):
        origin = me if origin is None else origin
        return pltpu.make_async_remote_copy(
            src_ref=spread.at[chunk, lax.rem(peer, shards), rows_of(0, peer // shards), :],
            dst_ref=returned.at[rows_of(chunk * tile, origin), :],
            send_sem=send_two.at[chunk, peer], recv_sem=recv_two.at[chunk, origin],
            device_id=device(peer), device_id_type=MESH)

    def around(mine, count, act):
        def turn(step, carry):
            act(lax.rem(mine + step, count))
            return carry

        lax.fori_loop(1, count, turn, 0)

    field_load.wait()
    first, second = field[:, :half], field[:, half:]
    field_high[0], field_low[0] = split(first + second)
    field_high[1], field_low[1] = split(first - second)
    kernel_load.wait()
    start_load.wait()
    source_load.wait()
    first, second = extra[:, :half], extra[:, half:]
    extra_high[0], extra_low[0] = split(first + second)
    extra_high[1], extra_low[1] = split(first - second)

    for chunk in range(chunks):
        which, offset = chunk // per_parity, chunk % per_parity * tile
        along[chunk * tile:(chunk + 1) * tile, :] = dot3(
            kernels[0, which, offset:offset + tile, :], kernels[1, which, offset:offset + tile, :],
            field_high[which], field_low[which], True)
        if chunk == 0:
            pl.semaphore_wait(barrier, group)

        @pl.when(has_guess)
        def _():
            around(me, group, lambda peer: first_copy(chunk, peer).start())

        mine = pl.ds(pl.multiple_of(offset + place * (shards * deep), shards * deep), shards * deep)
        along_extra[chunk] = dot3(
            kernels[0, which, mine, :], kernels[1, which, mine, :], extra_high[which], extra_low[which], True)
        around(space, shards, lambda shard: extra_copy(chunk, shard).start())

    for load in rows_loads:
        load.wait()
    columns_load.wait()
    owns = []
    for chunk in range(chunks):
        owns.append(pltpu.make_async_copy(
            along.at[rows_of(chunk * tile, me), :], gathered.at[chunk, space, rows_of(0, place), :],
            own_sem.at[0, chunk]))
        owns.append(pltpu.make_async_copy(
            along_extra.at[chunk, rows_of(0, space), :], gathered_extra.at[chunk, space], own_sem.at[1, chunk]))
    for own in owns:
        own.start()
    for own in owns:
        own.wait()

    lanes = 256
    across = length // lanes
    scale = 1.0 / float(length * length)

    def mix(chunk, first_side, index, carry):
        row = pl.multiple_of(index // across * 8, 8)
        lane = pl.ds(pl.multiple_of(lax.rem(index, across) * lanes, lanes), lanes)
        row_part = jnp.concatenate([row_sines[pl.ds(chunk * deep + row, 8), :]] * (lanes // 128), axis=1)
        stiffness = 4.0 * (column_sines[:, lane] + row_part)
        fine_factor = 1.0 / (1.0 + decay_rate + spread_rate * stiffness)
        coarse = 1.0 / (1.0 + M * decay_rate + M * spread_rate * stiffness)
        fine = fine_factor
        symbol = fine
        for _ in range(M - 1):
            fine = fine * fine_factor
            symbol = symbol + fine

        def at(turn):
            return pl.ds(pl.multiple_of(turn * deep + row, 8), 8)

        forcing = symbol * (scale * spectra[chunk, at(turns_here + 1), lane])
        gain = (fine * scale) * (fine - coarse)
        source_gain = (1.0 + fine - coarse) * forcing
        if first_side:
            before = fine * (scale * spectra[chunk, at(turns_here), lane]) + forcing
            state = fine * before + forcing
        else:
            before, state = incoming[chunk, at(0), lane], incoming[chunk, at(1), lane]
        states[chunk, at(0), lane] = before
        states[chunk, at(1), lane] = state
        for turn in range(2, turns_here + 2 if first_side else turns_here):
            state = coarse * state + (gain * spectra[chunk, at(turn - 2), lane] + source_gain)
            if turn < turns_here:
                states[chunk, at(turn), lane] = state
            else:
                crossing[chunk, at(turn - turns_here), lane] = state
        return carry

    steps = deep // 8 * across
    for chunk in range(chunks):
        def from_peer(peer):
            @pl.when(side * turns_here + peer // shards < turns - 2)
            def _():
                first_copy(chunk, me, peer).wait_recv()

        around(me, group, from_peer)
        around(space, shards, lambda shard: extra_copy(chunk, space, shard).wait_recv())
        for shard in range(shards // 2):
            columns = slice(shard * rows, (shard + 1) * rows)
            upper, lower = [
                jnp.concatenate(
                    [gathered[chunk, part], gathered_extra[chunk, part, :, :rows], gathered_extra[chunk, part, :, rows:]],
                    axis=0)
                for part in (shard, shard + shards // 2)
            ]
            sums_high[0, :, columns], sums_low[0, :, columns] = split(upper + lower)
            sums_high[1, :, columns], sums_low[1, :, columns] = split(upper - lower)
        for which in range(2):
            spectra[chunk, :, which * half:(which + 1) * half] = dot3(
                sums_high[which], sums_low[which], kernels[0, which], kernels[1, which], True)

        @pl.when(side == 0)
        def _():
            lax.fori_loop(0, steps, functools.partial(mix, chunk, True), 0)
            cross_copy(chunk).start()

    for chunk in range(chunks):
        @pl.when(side == 1)
        def _():
            cross_copy(chunk).wait_recv()
            lax.fori_loop(0, steps, functools.partial(mix, chunk, False), 0)

        even_high, even_low = split(states[chunk, :, :half])
        odd_high, odd_low = split(states[chunk, :, half:])
        for shard in range(shards // 2):
            columns = slice(shard * rows, (shard + 1) * rows)
            even = dot3(even_high, even_low, kernels[0, 0, :, columns], kernels[1, 0, :, columns])
            odd = dot3(odd_high, odd_low, kernels[0, 1, :, columns], kernels[1, 1, :, columns])
            spread[chunk, shard] = even + odd
            spread[chunk, shard + shards // 2] = even - odd
        around(me, group, lambda peer: second_copy(chunk, peer).start())
        own = pltpu.make_async_copy(
            spread.at[chunk, space, rows_of(0, place), :], returned.at[rows_of(chunk * tile, me), :],
            own_sem.at[2, chunk])
        own.start()
        own.wait()

    for chunk in range(chunks):
        around(me, group, lambda peer: second_copy(chunk, me, peer).wait_recv())
        which, offset = chunk // per_parity, chunk % per_parity * tile
        high, low = split(returned[chunk * tile:(chunk + 1) * tile, :].T)
        for index in range(0, half, 256):
            columns = slice(index, index + 256)
            opposite = slice(half + index, half + index + 256)
            value = dot3(
                high, low, kernels[0, which, offset:offset + tile, columns],
                kernels[1, which, offset:offset + tile, columns])
            if chunk == 0:
                field[:, columns] = value
            elif chunk < per_parity:
                field[:, columns] += value
            elif chunk < chunks - 1:
                if chunk == per_parity:
                    field[:, opposite] = value
                else:
                    field[:, opposite] += value
            else:
                odd = value if per_parity == 1 else field[:, opposite] + value
                even = field[:, columns]
                out_ref[0, :, columns] = even + odd
                out_ref[0, :, opposite] = even - odd

    for chunk in range(chunks):
        @pl.when(has_guess)
        def _():
            around(me, group, lambda peer: first_copy(chunk, peer).wait_send())

        around(space, shards, lambda shard: extra_copy(chunk, shard).wait_send())

        @pl.when(side == 0)
        def _():
            cross_copy(chunk).wait_send()

        around(me, group, lambda peer: second_copy(chunk, peer).wait_send())


def body(turns, shards, initial_guess, start_field, source_field):
    rows, length = start_field.shape
    group = turns * shards // 2
    half = length // 2
    chunks = min(4, length // group // 8)
    tile = length // chunks
    deep = tile // group
    slots = turns // 2 * deep
    kernels = jnp.asarray(half_kernels(length))
    sines = (np.sin(np.pi * mode_order(length) / length) ** 2).astype(np.float32)
    row_sines = jnp.asarray(np.repeat(sines[:, None], 128, axis=1))
    column_sines = jnp.asarray(np.repeat(sines[None, :], 8, axis=0))
    f32, bf16 = jnp.float32, jnp.bfloat16
    dma = pltpu.SemaphoreType.DMA
    return pl.pallas_call(
        functools.partial(mgrit_kernel, turns, shards, chunks),
        out_shape=jax.ShapeDtypeStruct(initial_guess.shape, f32),
        in_specs=[pl.BlockSpec(memory_space=pltpu.HBM)] * 6,
        out_specs=pl.BlockSpec(memory_space=pltpu.VMEM),
        scratch_shapes=[
            pltpu.VMEM((rows, length), f32),
            pltpu.VMEM((2 * rows, length), f32),
            pltpu.VMEM((2, 2, half, half), bf16),
            pltpu.VMEM((chunks * deep, 128), f32),
            pltpu.VMEM((8, length), f32),
            pltpu.VMEM((2, rows, half), bf16),
            pltpu.VMEM((2, rows, half), bf16),
            pltpu.VMEM((2, 2 * rows, half), bf16),
            pltpu.VMEM((2, 2 * rows, half), bf16),
            pltpu.VMEM((2, slots + 2 * deep, half), bf16),
            pltpu.VMEM((2, slots + 2 * deep, half), bf16),
            pltpu.VMEM((length, rows), f32),
            pltpu.VMEM((chunks, shards * deep, 2 * rows), f32),
            pltpu.VMEM((chunks, shards, slots, rows), f32),
            pltpu.VMEM((chunks, shards, deep, 2 * rows), f32),
            pltpu.VMEM((chunks, slots + 2 * deep, length), f32),
            pltpu.VMEM((chunks, slots, length), f32),
            pltpu.VMEM((chunks, 2 * deep, length), f32),
            pltpu.VMEM((chunks, 2 * deep, length), f32),
            pltpu.VMEM((chunks, shards, slots, rows), f32),
            pltpu.VMEM((length, rows), f32),
            dma((3,)), dma, dma((chunks,)), dma, dma((chunks, group)), dma((chunks, group)),
            dma((chunks, shards)), dma((chunks, shards)), dma((chunks,)), dma((chunks,)),
            dma((chunks, group)), dma((chunks, group)), dma((3, chunks)),
        ],
        compiler_params=pltpu.CompilerParams(
            collective_id=0, has_side_effects=True, vmem_limit_bytes=40 * 1024 * 1024),
    )(*(pltpu.with_memory_space_constraint(value, pltpu.HBM)
        for value in (initial_guess, start_field, source_field, kernels, row_sines, column_sines)))


def solution(mesh):
    return jax.shard_map(
        functools.partial(body, mesh.shape["tm"], mesh.shape["space"]),
        mesh=mesh,
        in_specs=(P("tm", "space", None), P("space", None), P("space", None)),
        out_specs=P("tm", "space", None),
        check_vma=False,
    )
```

```python
import functools

import jax
import jax.numpy as jnp
import numpy as np
from jax import lax
from jax.experimental import pallas as pl
from jax.experimental.pallas import tpu as pltpu
from jax.sharding import PartitionSpec as P

M = 16
MESH = pl.DeviceIdType.MESH

decay_rate = 0.0005
spread_rate = 0.01


def mode_order(length):
    return np.concatenate([np.arange(0, length, 2), np.arange(1, length, 2)])


def half_kernels(length):
    half = length // 2
    product = mode_order(length)[:, None] * np.arange(half)[None, :] % length
    angles = 2.0 * np.pi / length * product
    full = (np.cos(angles) + np.sin(angles)).astype(np.float32).reshape(2, half, half)
    high = full.astype(jnp.bfloat16)
    low = (full - high.astype(np.float32)).astype(jnp.bfloat16)
    return np.stack([high, low])


def split(value):
    high = value.astype(jnp.bfloat16)
    low = (value - high.astype(jnp.float32)).astype(jnp.bfloat16)
    return high, low


def dot(a, b, transposed):
    dims = (((1,), (1 if transposed else 0,)), ((), ()))
    return lax.dot_general(a, b, dims, preferred_element_type=jnp.float32)


def dot3(a_high, a_low, b_high, b_low, transposed=False):
    return (
        dot(a_high, b_high, transposed)
        + (dot(a_low, b_high, transposed) + dot(a_high, b_low, transposed))
    )


def mgrit_kernel(
    turns, shards, chunks,
    guess, start, source, kernels_hbm, rows_hbm, columns_hbm, out_ref,
    field, extra, kernels, row_sines, column_sines, field_high, field_low, extra_high, extra_low,
    sums_high, sums_low, along, along_extra, gathered, gathered_extra, spectra, states, crossing, incoming,
    spread, returned,
    load_sem, kernel_sem, rows_sem, columns_sem, send_one, recv_one, send_extra, recv_extra,
    send_cross, recv_cross, send_two, recv_two, own_sem,
):
    tm, space = lax.axis_index("tm"), lax.axis_index("space")
    devices = turns * shards
    group = devices // 2
    turns_here = turns // 2
    side = tm // turns_here
    place = lax.rem(tm, turns_here)
    me = place * shards + space
    rows, length = field.shape
    half = length // 2
    tile = length // chunks
    deep = tile // group
    slots = turns_here * deep
    per_parity = chunks // 2
    has_guess = tm < turns - 2

    field_load = pltpu.make_async_copy(guess.at[0], field, load_sem.at[0])
    field_load.start()
    kernel_load = pltpu.make_async_copy(kernels_hbm, kernels, kernel_sem)
    kernel_load.start()
    start_load = pltpu.make_async_copy(start, extra.at[pl.ds(0, rows), :], load_sem.at[1])
    start_load.start()
    source_load = pltpu.make_async_copy(source, extra.at[pl.ds(rows, rows), :], load_sem.at[2])
    source_load.start()
    rows_loads = []
    for chunk in range(chunks):
        load = pltpu.make_async_copy(
            rows_hbm.at[pl.ds(pl.multiple_of(chunk * tile + me * deep, deep), deep), :],
            row_sines.at[pl.ds(chunk * deep, deep), :], rows_sem.at[chunk])
        load.start()
        rows_loads.append(load)
    columns_load = pltpu.make_async_copy(columns_hbm, column_sines, columns_sem)
    columns_load.start()

    def device(peer):
        return (side * turns_here + peer // shards, lax.rem(peer, shards))

    other = (lax.rem(tm + turns_here, turns), space)
    barrier = pltpu.get_barrier_semaphore()

    def greet(step, carry):
        pl.semaphore_signal(barrier, inc=1, device_id=device(lax.rem(me + step, group)), device_id_type=MESH)
        return carry

    lax.fori_loop(1, group, greet, 0)
    pl.semaphore_signal(barrier, inc=1, device_id=other, device_id_type=MESH)

    def rows_of(base, index):
        return pl.ds(pl.multiple_of(base + index * deep, deep), deep)

    def first_copy(chunk, peer, origin=None):
        origin = me if origin is None else origin
        return pltpu.make_async_remote_copy(
            src_ref=along.at[rows_of(chunk * tile, peer), :],
            dst_ref=gathered.at[chunk, lax.rem(origin, shards), rows_of(0, origin // shards), :],
            send_sem=send_one.at[chunk, peer], recv_sem=recv_one.at[chunk, origin],
            device_id=device(peer), device_id_type=MESH)

    def extra_copy(chunk, shard, origin=None):
        origin = space if origin is None else origin
        return pltpu.make_async_remote_copy(
            src_ref=along_extra.at[chunk, rows_of(0, shard), :],
            dst_ref=gathered_extra.at[chunk, origin],
            send_sem=send_extra.at[chunk, shard], recv_sem=recv_extra.at[chunk, origin],
            device_id=(tm, shard), device_id_type=MESH)

    def cross_copy(chunk):
        return pltpu.make_async_remote_copy(
            src_ref=crossing.at[chunk], dst_ref=incoming.at[chunk],
            send_sem=send_cross.at[chunk], recv_sem=recv_cross.at[chunk],
            device_id=other, device_id_type=MESH)

    def second_copy(chunk, peer, origin=None):
        origin = me if origin is None else origin
        return pltpu.make_async_remote_copy(
            src_ref=spread.at[chunk, lax.rem(peer, shards), rows_of(0, peer // shards), :],
            dst_ref=returned.at[rows_of(chunk * tile, origin), :],
            send_sem=send_two.at[chunk, peer], recv_sem=recv_two.at[chunk, origin],
            device_id=device(peer), device_id_type=MESH)

    def around(mine, count, act):
        def turn(step, carry):
            act(lax.rem(mine + step, count))
            return carry

        lax.fori_loop(1, count, turn, 0)

    field_load.wait()
    first, second = field[:, :half], field[:, half:]
    field_high[0], field_low[0] = split(first + second)
    field_high[1], field_low[1] = split(first - second)
    kernel_load.wait()

    for chunk in range(chunks):
        which, offset = chunk // per_parity, chunk % per_parity * tile
        along[chunk * tile:(chunk + 1) * tile, :] = dot3(
            kernels[0, which, offset:offset + tile, :], kernels[1, which, offset:offset + tile, :],
            field_high[which], field_low[which], True)
        if chunk == 0:
            pl.semaphore_wait(barrier, group)

        @pl.when(has_guess)
        def _():
            around(me, group, lambda peer: first_copy(chunk, peer).start())

        if chunk == 0:
            start_load.wait()
            source_load.wait()
            first, second = extra[:, :half], extra[:, half:]
            extra_high[0], extra_low[0] = split(first + second)
            extra_high[1], extra_low[1] = split(first - second)
        mine = pl.ds(pl.multiple_of(offset + place * (shards * deep), shards * deep), shards * deep)
        along_extra[chunk] = dot3(
            kernels[0, which, mine, :], kernels[1, which, mine, :], extra_high[which], extra_low[which], True)
        around(space, shards, lambda shard: extra_copy(chunk, shard).start())

    for load in rows_loads:
        load.wait()
    columns_load.wait()
    owns = []
    for chunk in range(chunks):
        owns.append(pltpu.make_async_copy(
            along.at[rows_of(chunk * tile, me), :], gathered.at[chunk, space, rows_of(0, place), :],
            own_sem.at[0, chunk]))
        owns.append(pltpu.make_async_copy(
            along_extra.at[chunk, rows_of(0, space), :], gathered_extra.at[chunk, space], own_sem.at[1, chunk]))
    for own in owns:
        own.start()
    for own in owns:
        own.wait()

    lanes = 256
    across = length // lanes
    scale = 1.0 / float(length * length)

    def mix(chunk, first_side, index, carry):
        row = pl.multiple_of(index // across * 8, 8)
        lane = pl.ds(pl.multiple_of(lax.rem(index, across) * lanes, lanes), lanes)
        row_part = jnp.concatenate([row_sines[pl.ds(chunk * deep + row, 8), :]] * (lanes // 128), axis=1)
        stiffness = 4.0 * (column_sines[:, lane] + row_part)
        fine_factor = 1.0 / (1.0 + decay_rate + spread_rate * stiffness)
        coarse = 1.0 / (1.0 + M * decay_rate + M * spread_rate * stiffness)
        fine = fine_factor
        symbol = fine
        for _ in range(M - 1):
            fine = fine * fine_factor
            symbol = symbol + fine

        def at(turn):
            return pl.ds(pl.multiple_of(turn * deep + row, 8), 8)

        forcing = symbol * (scale * spectra[chunk, at(turns_here + 1), lane])
        gain = (fine * scale) * (fine - coarse)
        source_gain = (1.0 + fine - coarse) * forcing
        if first_side:
            before = fine * (scale * spectra[chunk, at(turns_here), lane]) + forcing
            state = fine * before + forcing
        else:
            before, state = incoming[chunk, at(0), lane], incoming[chunk, at(1), lane]
        states[chunk, at(0), lane] = before
        states[chunk, at(1), lane] = state
        for turn in range(2, turns_here + 2 if first_side else turns_here):
            state = coarse * state + (gain * spectra[chunk, at(turn - 2), lane] + source_gain)
            if turn < turns_here:
                states[chunk, at(turn), lane] = state
            else:
                crossing[chunk, at(turn - turns_here), lane] = state
        return carry

    steps = deep // 8 * across
    for chunk in range(chunks):
        def from_peer(peer):
            @pl.when(side * turns_here + peer // shards < turns - 2)
            def _():
                first_copy(chunk, me, peer).wait_recv()

        around(me, group, from_peer)
        around(space, shards, lambda shard: extra_copy(chunk, space, shard).wait_recv())
        for shard in range(shards // 2):
            columns = slice(shard * rows, (shard + 1) * rows)
            upper, lower = [
                jnp.concatenate(
                    [gathered[chunk, part], gathered_extra[chunk, part, :, :rows], gathered_extra[chunk, part, :, rows:]],
                    axis=0)
                for part in (shard, shard + shards // 2)
            ]
            sums_high[0, :, columns], sums_low[0, :, columns] = split(upper + lower)
            sums_high[1, :, columns], sums_low[1, :, columns] = split(upper - lower)
        for which in range(2):
            spectra[chunk, :, which * half:(which + 1) * half] = dot3(
                sums_high[which], sums_low[which], kernels[0, which], kernels[1, which], True)

        @pl.when(side == 0)
        def _():
            lax.fori_loop(0, steps, functools.partial(mix, chunk, True), 0)
            cross_copy(chunk).start()

    for chunk in range(chunks):
        @pl.when(side == 1)
        def _():
            cross_copy(chunk).wait_recv()
            lax.fori_loop(0, steps, functools.partial(mix, chunk, False), 0)

        even_high, even_low = split(states[chunk, :, :half])
        odd_high, odd_low = split(states[chunk, :, half:])
        for shard in range(shards // 2):
            columns = slice(shard * rows, (shard + 1) * rows)
            even = dot3(even_high, even_low, kernels[0, 0, :, columns], kernels[1, 0, :, columns])
            odd = dot3(odd_high, odd_low, kernels[0, 1, :, columns], kernels[1, 1, :, columns])
            spread[chunk, shard] = even + odd
            spread[chunk, shard + shards // 2] = even - odd
        around(me, group, lambda peer: second_copy(chunk, peer).start())
        own = pltpu.make_async_copy(
            spread.at[chunk, space, rows_of(0, place), :], returned.at[rows_of(chunk * tile, me), :],
            own_sem.at[2, chunk])
        own.start()
        own.wait()

    for chunk in range(chunks):
        around(me, group, lambda peer: second_copy(chunk, me, peer).wait_recv())
        which, offset = chunk // per_parity, chunk % per_parity * tile
        high, low = split(returned[chunk * tile:(chunk + 1) * tile, :].T)
        for index in range(0, half, 256):
            columns = slice(index, index + 256)
            opposite = slice(half + index, half + index + 256)
            value = dot3(
                high, low, kernels[0, which, offset:offset + tile, columns],
                kernels[1, which, offset:offset + tile, columns])
            if chunk == 0:
                field[:, columns] = value
            elif chunk < per_parity:
                field[:, columns] += value
            elif chunk < chunks - 1:
                if chunk == per_parity:
                    field[:, opposite] = value
                else:
                    field[:, opposite] += value
            else:
                odd = value if per_parity == 1 else field[:, opposite] + value
                even = field[:, columns]
                out_ref[0, :, columns] = even + odd
                out_ref[0, :, opposite] = even - odd

    for chunk in range(chunks):
        @pl.when(has_guess)
        def _():
            around(me, group, lambda peer: first_copy(chunk, peer).wait_send())

        around(space, shards, lambda shard: extra_copy(chunk, shard).wait_send())

        @pl.when(side == 0)
        def _():
            cross_copy(chunk).wait_send()

        around(me, group, lambda peer: second_copy(chunk, peer).wait_send())


def body(turns, shards, initial_guess, start_field, source_field):
    rows, length = start_field.shape
    group = turns * shards // 2
    half = length // 2
    chunks = min(4, length // group // 8)
    tile = length // chunks
    deep = tile // group
    slots = turns // 2 * deep
    kernels = jnp.asarray(half_kernels(length))
    sines = (np.sin(np.pi * mode_order(length) / length) ** 2).astype(np.float32)
    row_sines = jnp.asarray(np.repeat(sines[:, None], 128, axis=1))
    column_sines = jnp.asarray(np.repeat(sines[None, :], 8, axis=0))
    f32, bf16 = jnp.float32, jnp.bfloat16
    dma = pltpu.SemaphoreType.DMA
    return pl.pallas_call(
        functools.partial(mgrit_kernel, turns, shards, chunks),
        out_shape=jax.ShapeDtypeStruct(initial_guess.shape, f32),
        in_specs=[pl.BlockSpec(memory_space=pltpu.HBM)] * 6,
        out_specs=pl.BlockSpec(memory_space=pltpu.VMEM),
        scratch_shapes=[
            pltpu.VMEM((rows, length), f32),
            pltpu.VMEM((2 * rows, length), f32),
            pltpu.VMEM((2, 2, half, half), bf16),
            pltpu.VMEM((chunks * deep, 128), f32),
            pltpu.VMEM((8, length), f32),
            pltpu.VMEM((2, rows, half), bf16),
            pltpu.VMEM((2, rows, half), bf16),
            pltpu.VMEM((2, 2 * rows, half), bf16),
            pltpu.VMEM((2, 2 * rows, half), bf16),
            pltpu.VMEM((2, slots + 2 * deep, half), bf16),
            pltpu.VMEM((2, slots + 2 * deep, half), bf16),
            pltpu.VMEM((length, rows), f32),
            pltpu.VMEM((chunks, shards * deep, 2 * rows), f32),
            pltpu.VMEM((chunks, shards, slots, rows), f32),
            pltpu.VMEM((chunks, shards, deep, 2 * rows), f32),
            pltpu.VMEM((chunks, slots + 2 * deep, length), f32),
            pltpu.VMEM((chunks, slots, length), f32),
            pltpu.VMEM((chunks, 2 * deep, length), f32),
            pltpu.VMEM((chunks, 2 * deep, length), f32),
            pltpu.VMEM((chunks, shards, slots, rows), f32),
            pltpu.VMEM((length, rows), f32),
            dma((3,)), dma, dma((chunks,)), dma, dma((chunks, group)), dma((chunks, group)),
            dma((chunks, shards)), dma((chunks, shards)), dma((chunks,)), dma((chunks,)),
            dma((chunks, group)), dma((chunks, group)), dma((3, chunks)),
        ],
        compiler_params=pltpu.CompilerParams(
            collective_id=0, has_side_effects=True, vmem_limit_bytes=40 * 1024 * 1024),
    )(*(pltpu.with_memory_space_constraint(value, pltpu.HBM)
        for value in (initial_guess, start_field, source_field, kernels, row_sines, column_sines)))


def solution(mesh):
    return jax.shard_map(
        functools.partial(body, mesh.shape["tm"], mesh.shape["space"]),
        mesh=mesh,
        in_specs=(P("tm", "space", None), P("space", None), P("space", None)),
        out_specs=P("tm", "space", None),
        check_vma=False,
    )
```
